32 devices in a mesh: ep: 8 (over z, y), tp: 4 (over x, core).
Axes of the slice: x: 2, y: 2, z: 4, core: 2. Of those that a mesh axis runs over, the one named last changes fastest.
Arguments:
- tokens_first: bfloat16 [384, 2048], P('ep', 'tp'), may hold values from -6 to 6
- routes_first: int32 [384, 8], P('ep'), may hold values from 0 to 63, all different within a row; in each aligned block of 48 rows (0 to 47, 48 to 95, ...) at most 12 rows name the same one
- weights_first: float32 [384, 8], P('ep'), may hold values from 0.05 to 1
- tokens_second: bfloat16 [384, 2048], P('ep', 'tp'), may hold values from -6 to 6
- stream_second: bfloat16 [384, 2048], P('ep', 'tp'), may hold values from -6 to 6
- routes_second: int32 [384, 8], P('ep'), may hold values from 0 to 63, all different within a row; in each aligned block of 48 rows (0 to 47, 48 to 95, ...) at most 12 rows name the same one
- weights_second: float32 [384, 8], P('ep'), may hold values from 0.05 to 1
- old_place: int32 [64], replicated, may hold values from 0 to 63, each once
- new_place: int32 [72], replicated, may hold values from 0 to 63, as said below
- gate_up: bfloat16 [64, 2, 2048, 1024], P('ep', None, None, 'tp'), may hold values from -0.125 to 0.125
- down_proj: bfloat16 [64, 1024, 2048], P('ep', 'tp'), may hold values from -0.1875 to 0.1875
- attn_gain: float32 [2048], P('tp'), may hold values from 0.25 to 1.75
- qkv_weight: bfloat16 [2048, 3, 2048], P(None, None, 'tp'), may hold values from -0.125 to 0.125
- query_gain: float32 [128], replicated, may hold values from 0.25 to 1.75
- key_gain: float32 [128], replicated, may hold values from 0.25 to 1.75
- positions: int32 [384], P('ep'), may hold values from 0 to 4095
Outputs:
- output_first: bfloat16 [384, 2048], P('ep', 'tp')
- query_rows: bfloat16 [384, 2048], P('ep', 'tp')
- key_rows: bfloat16 [384, 2048], P('ep', 'tp')
- value_rows: bfloat16 [384, 2048], P('ep', 'tp')
- new_gate_up: bfloat16 [72, 2, 2048, 1024], P('ep', None, None, 'tp')
- new_down: bfloat16 [72, 1024, 2048], P('ep', 'tp')
The draws below stay inside these ranges and needn't reach their ends.
Inputs may be any that keep to these rules, and one draw needn't show every extreme that they name: `routes_first`: within the 48 rows of one index of ep, no expert is named more than 12 times, a bound that some block reaches. `routes_second`: within the 48 rows of one index of ep, no expert is named more than 12 times, a bound that some block reaches. `old_place`: each expert is held by exactly one slot. `new_place`: slots s * 9 to s * 9 + 8 belong to index s of ep; every expert is held by at least one slot, and some by two or more.
All inputs are finite; a program needn't handle non-finite values.
Results may differ from the reference program's by a relative error of at most 0.017.
Values may be sent and summed in bfloat16 or wider, within the bound.
A program may use at most 192 MiB of HBM per device.

```python
import math
import jax
import jax.numpy as jnp
import numpy as np
from jax import lax

D = 2048
FF = 1024
EXPERTS = 64
TOP = 8
HEADS = 16
HEAD_DIM = 128
TOK_DEV = 48
CAP = 12
NEW_DEV = 9
NEW_SLOTS = 72
TOKENS = 384
N_EP = 8
N_TP = 4


def draw_new_place(key, part):
    groups = NEW_SLOTS // NEW_DEV
    first_key, second_key, third_key = jax.random.split(jax.random.fold_in(key, 17), 3)
    base = jax.random.permutation(first_key, EXPERTS).astype(jnp.int32).reshape(groups, NEW_DEV - 1)
    extra = jax.random.randint(second_key, (groups, 1), 0, EXPERTS, dtype=jnp.int32)
    table = jnp.concatenate([base, extra], axis=1)
    offset = jax.random.randint(third_key, (groups, 1), 0, NEW_DEV, dtype=jnp.int32)
    order = (jnp.arange(NEW_DEV, dtype=jnp.int32)[None, :] + offset) % NEW_DEV
    return jnp.take_along_axis(table, order, axis=1).reshape(-1)


def place_ends(drawn, rng, smallest, high):
    place = [jax.random.randint(jax.random.fold_in(rng, axis), (), 0, length) for axis, length in enumerate(drawn.shape)]
    main_axis = drawn.shape.index(max(drawn.shape))
    neighbour = place[:main_axis] + [(place[main_axis] + 1) % drawn.shape[main_axis]] + place[main_axis + 1:]
    return drawn.at[tuple(place)].set(smallest).at[tuple(neighbour)].set(high)


def shard_levels(own_key, extent, cuts, low, top_value):
    def one(dim, blocks):
        steps = jax.random.uniform(jax.random.fold_in(jax.random.fold_in(own_key, 6), dim), (blocks,), jnp.float32, low / len(cuts), top_value / len(cuts))
        return jnp.repeat(jnp.exp(steps), extent[dim] // blocks).reshape((-1,) + (1,) * (len(extent) - dim - 1))

    factor_of = one(*cuts[0])
    for cut in cuts[1:]:
        factor_of = factor_of * one(*cut)
    return factor_of


def routed_block(own_key, own, number, rows, count, top, reach, lean):
    sequence = jax.random.permutation(own_key, count)
    packed, ordinary = load_shares(count, rows * top, reach, lean, True), load_shares(count, rows * top, reach, lean, False)
    places = jnp.arange(count)

    def named(lengths, turn):
        used = int((lengths > 0).sum())
        fixed = max(1, used // 4)
        shifted = fixed + (places - fixed + turn * (used - fixed)) % max(1, count - fixed)
        return jnp.zeros((count,), jnp.int32).at[sequence[jnp.where(places < fixed, places, shifted)]].set(jnp.asarray(lengths, jnp.int32))

    lengths = jnp.where(number % 4 == 0, named(packed, number // 4), named(ordinary, number - number // 4 - 1))
    mixed = jax.random.permutation(jax.random.fold_in(own, 3), count)
    donor, taker = mixed[0:count // 2 * 2:2], mixed[1:count // 2 * 2:2]
    margin = jnp.minimum(lengths[donor] - 1, reach - lengths[taker]) // 2
    margin = jnp.where((donor == sequence[0]) | (taker == sequence[0]) | (lengths[taker] == 0), 0, jnp.maximum(margin, 0))
    shifted = jax.random.randint(jax.random.fold_in(own, 4), (count // 2,), 0, 1 << 20) % (margin + 1)
    lengths = lengths.at[donor].add(-shifted).at[taker].add(shifted)
    labels = jnp.searchsorted(jnp.cumsum(lengths), jnp.arange(rows * top), side="right").astype(jnp.int32)
    table = labels.reshape(top, rows).T
    table = table[jax.random.permutation(jax.random.fold_in(own, 1), rows)]
    turn = jax.random.randint(jax.random.fold_in(own, 2), (rows, 1), 0, top)
    return jnp.take_along_axis(table, (jnp.arange(top)[None, :] + turn) % top, axis=1)


def load_shares(amount, total, reach, lean, full):
    loads = [(1 << 20) // math.isqrt(standing ** lean) + 1 for standing in range(1, amount + 1)]
    largest = reach if full else min(reach, max(-(-total // amount), total * loads[0] // sum(loads)))
    least = 1 if total - largest >= amount - 1 else 0
    given, surplus = [largest] + [least] * (amount - 1), total - largest - least * (amount - 1)
    while surplus > 0:
        movable = [i for i in range(1, amount) if given[i] < largest] or [i for i in range(1, amount) if given[i] < reach]
        whole, left = sum([loads[i] for i in movable]), surplus
        for i in movable:
            more = min(reach - given[i], max(1, left * loads[i] // whole), surplus)
            given[i] = given[i] + more
            surplus = surplus - more
    return np.array(given)


def noise(stream_key, dims, spread, reach, cuts=(), kind=jnp.bfloat16):
    entries = jax.random.normal(stream_key, dims, jnp.float32) * spread
    if len(cuts) > 0:
        entries = shard_levels(stream_key, dims, cuts, -0.22, 0.18) * entries
    return jnp.clip(entries, min=-reach, max=reach).astype(kind)


def setup_inputs(seed: int = 0) -> dict:
    keys = jax.random.split(jax.random.key(seed), 17)
    tokens_first = noise(keys[0], (TOKENS, D), 1.0, 6.0, ((0, 8), (1, 4)))
    routes_first_keys = jax.random.split(jax.random.fold_in(keys[1], 1), TOKENS // TOK_DEV)
    routes_first_turns = jax.random.permutation(jax.random.fold_in(keys[1], 3), TOKENS // TOK_DEV)
    routes_first = jax.vmap(lambda own, number: routed_block(jax.random.fold_in(keys[1], 2), own, number, TOK_DEV, EXPERTS, TOP, CAP, 2))(routes_first_keys, routes_first_turns).reshape((TOKENS, TOP))
    weights_first = jnp.clip(jnp.exp(math.log(1.0) - 2.9957323 * jax.random.uniform(keys[2], (TOKENS, TOP), jnp.float32) ** shard_levels(keys[2], (TOKENS, TOP), ((0, 8),), -0.2, 0.2)), 0.05, 1.0)
    tokens_second = noise(keys[3], (TOKENS, D), 1.0, 6.0, ((0, 8), (1, 4)))
    stream_second = noise(keys[4], (TOKENS, D), 1.0, 6.0, ((0, 8), (1, 4)))
    routes_second_keys = jax.random.split(jax.random.fold_in(keys[5], 1), TOKENS // TOK_DEV)
    routes_second_turns = jax.random.permutation(jax.random.fold_in(keys[5], 3), TOKENS // TOK_DEV)
    routes_second = jax.vmap(lambda own, number: routed_block(jax.random.fold_in(keys[5], 2), own, number, TOK_DEV, EXPERTS, TOP, CAP, 2))(routes_second_keys, routes_second_turns).reshape((TOKENS, TOP))
    weights_second = jnp.clip(jnp.exp(math.log(1.0) - 2.9957323 * jax.random.uniform(keys[6], (TOKENS, TOP), jnp.float32) ** shard_levels(keys[6], (TOKENS, TOP), ((0, 8),), -0.2, 0.2)), 0.05, 1.0)
    old_place = jax.random.permutation(keys[7], EXPERTS).astype(jnp.int32)
    new_place = draw_new_place(jax.random.fold_in(keys[16], 71), 0)
    gate_up = noise(keys[9], (EXPERTS, 2, D, FF), D ** -0.5, 0.125, ((0, 8), (3, 4)))
    down_proj = noise(keys[10], (EXPERTS, FF, D), FF ** -0.5, 0.1875, ((0, 8), (1, 4)))
    attn_gain = jnp.clip(1.0 + 0.15 * jax.random.normal(keys[11], (D,), jnp.float32), 0.25, 1.75)
    qkv_weight = noise(keys[12], (D, 3, HEADS * HEAD_DIM), D ** -0.5, 0.125, ((2, 4),))
    query_gain = jnp.clip(1.0 + 0.15 * jax.random.normal(keys[13], (HEAD_DIM,), jnp.float32), 0.25, 1.75)
    key_gain = jnp.clip(1.0 + 0.15 * jax.random.normal(keys[14], (HEAD_DIM,), jnp.float32), 0.25, 1.75)
    positions = place_ends(jax.random.randint(keys[15], (TOKENS,), 0, 4096), jax.random.fold_in(keys[15], 1), 0, 4095).astype(jnp.int32)
    return {"tokens_first": tokens_first, "routes_first": routes_first, "weights_first": weights_first, "tokens_second": tokens_second, "stream_second": stream_second, "routes_second": routes_second, "weights_second": weights_second, "old_place": old_place, "new_place": new_place, "gate_up": gate_up, "down_proj": down_proj, "attn_gain": attn_gain, "qkv_weight": qkv_weight, "query_gain": query_gain, "key_gain": key_gain, "positions": positions}


def expert_rows(tokens, routes, gate_up, down_proj, old_slot):
    total_rows = routes.shape[0] * routes.shape[1]
    flattened = routes.reshape(-1)
    padded = jnp.concatenate([tokens, jnp.zeros((1, D), jnp.bfloat16)], axis=0)
    most_rows = N_EP * CAP

    def per_expert(expert):
        found_rows = jnp.nonzero(flattened == expert, size=most_rows, fill_value=total_rows)[0].astype(jnp.int32)
        picked = padded[found_rows // TOP]
        slot_index = old_slot[expert]
        gate_slot = lax.dynamic_index_in_dim(gate_up, slot_index, 0, keepdims=False)
        down_slot = lax.dynamic_index_in_dim(down_proj, slot_index, 0, keepdims=False)
        gate_part = jnp.dot(picked, gate_slot[0], preferred_element_type=jnp.float32)
        up_part = jnp.dot(picked, gate_slot[1], preferred_element_type=jnp.float32)
        hidden = (jax.nn.silu(gate_part) * up_part).astype(jnp.bfloat16)
        blocks = jnp.einsum('rjf,jfd->jrd', hidden.reshape(most_rows, N_TP, FF // N_TP).astype(jnp.float32), down_slot.reshape(N_TP, FF // N_TP, D).astype(jnp.float32))
        result = lax.optimization_barrier(jnp.sum(blocks.astype(jnp.bfloat16).astype(jnp.float32), axis=0)).astype(jnp.bfloat16)
        return (found_rows, result)
    found_rows, results = lax.map(per_expert, jnp.arange(EXPERTS, dtype=jnp.int32))
    gathered = jnp.zeros((total_rows + 1, D), jnp.bfloat16).at[found_rows.reshape(-1)].set(results.reshape(-1, D))
    return gathered[:total_rows]

def mixture(tokens, routes, weights, gate_up, down_proj, old_slot):
    rows_out = expert_rows(tokens, routes, gate_up, down_proj, old_slot)
    picked = rows_out.reshape(routes.shape[0], routes.shape[1], D).astype(jnp.float32)
    shares = weights / lax.optimization_barrier(jnp.sum(weights, axis=1, keepdims=True))
    return lax.optimization_barrier(jnp.sum(picked * shares[:, :, None], axis=1))

def head_norm(values, gain):
    mean_sq = lax.optimization_barrier(jnp.mean(values * values, axis=-1, keepdims=True))
    return values * lax.rsqrt(mean_sq + 1e-06) * gain

def apply_rope(values, positions):
    half = HEAD_DIM // 2
    inverse = jnp.exp(jnp.arange(half, dtype=jnp.float32) * (-2.0 / HEAD_DIM) * math.log(50000.0))
    angle = positions.astype(jnp.float32)[:, None] * inverse[None, :]
    cosine = jnp.cos(angle)[:, None, :]
    sine = jnp.sin(angle)[:, None, :]
    first = values[..., :half]
    second = values[..., half:]
    return jnp.concatenate([first * cosine - second * sine, second * cosine + first * sine], axis=-1)

def reference(tokens_first, routes_first, weights_first, tokens_second, stream_second, routes_second, weights_second, old_place, new_place, gate_up, down_proj, attn_gain, qkv_weight, query_gain, key_gain, positions):
    old_slot = jnp.zeros((EXPERTS,), jnp.int32).at[old_place].set(jnp.arange(EXPERTS, dtype=jnp.int32))
    source = old_slot[new_place]
    new_gate_up = gate_up[source]
    new_down = down_proj[source]
    output_first = mixture(tokens_first, routes_first, weights_first, gate_up, down_proj, old_slot).astype(jnp.bfloat16)
    stream = stream_second.astype(jnp.float32) + mixture(tokens_second, routes_second, weights_second, gate_up, down_proj, old_slot)
    mean_sq = lax.optimization_barrier(jnp.mean(stream * stream, axis=1, keepdims=True))
    normed = (stream * lax.rsqrt(mean_sq + 1e-06) * attn_gain[None, :]).astype(jnp.bfloat16)
    tokens_count = normed.shape[0]
    query_part = jnp.dot(normed, qkv_weight[:, 0, :], preferred_element_type=jnp.float32)
    key_part = jnp.dot(normed, qkv_weight[:, 1, :], preferred_element_type=jnp.float32)
    value_part = jnp.dot(normed, qkv_weight[:, 2, :], preferred_element_type=jnp.float32)
    query_heads = head_norm(query_part.reshape(tokens_count, HEADS, HEAD_DIM), query_gain)
    key_heads = head_norm(key_part.reshape(tokens_count, HEADS, HEAD_DIM), key_gain)
    query_rows = apply_rope(query_heads, positions).reshape(tokens_count, -1).astype(jnp.bfloat16)
    key_rows = apply_rope(key_heads, positions).reshape(tokens_count, -1).astype(jnp.bfloat16)
    value_rows = value_part.astype(jnp.bfloat16)
    return (output_first, query_rows, key_rows, value_rows, new_gate_up, new_down)
```

```python
import math

import jax
import jax.numpy as jnp
from jax import lax
from jax.experimental import pallas as pl
from jax.experimental.pallas import tpu as pltpu
from jax.sharding import PartitionSpec as P

D = 2048
EXPERTS = 64
HEAD_DIM = 128


def expert_body(x_ref, share_ref, gate_up_ref, down_ref, out_ref, total):
    slot = pl.program_id(1)

    @pl.when(slot == 0)
    def _():
        total[...] = jnp.zeros_like(total)

    rows = 256 if x_ref.shape[0] % 256 == 0 else 48

    def step(i, carry):
        at = pl.ds(pl.multiple_of(i * rows, rows), rows)
        x = x_ref[at, :]
        gate_part = jnp.dot(x, gate_up_ref[0, 0], preferred_element_type=jnp.float32)
        up_part = jnp.dot(x, gate_up_ref[0, 1], preferred_element_type=jnp.float32)
        hidden = gate_part / (1.0 + jnp.exp(-gate_part)) * up_part * share_ref[0, at, :]
        total[at, :] += jnp.dot(
            hidden.astype(jnp.bfloat16), down_ref[0], preferred_element_type=jnp.float32
        )
        return carry

    lax.fori_loop(0, x_ref.shape[0] // rows, step, 0)

    @pl.when(slot == pl.num_programs(1) - 1)
    def _():
        out_ref[...] = total[...].astype(jnp.bfloat16)


def expert_sums(x, shares, gate_up, down_proj):
    count, width = x.shape
    slots, _, _, units = gate_up.shape
    block = 768 if count % 768 == 0 else count
    return pl.pallas_call(
        expert_body,
        grid=(count // block, slots),
        in_specs=[
            pl.BlockSpec((block, width), lambda i, s: (i, 0)),
            pl.BlockSpec((1, block, 1), lambda i, s: (s, i, 0)),
            pl.BlockSpec((1, 2, width, units), lambda i, s: (s, 0, 0, 0)),
            pl.BlockSpec((1, units, width), lambda i, s: (s, 0, 0)),
        ],
        out_specs=pl.BlockSpec((block, width), lambda i, s: (i, 0)),
        out_shape=jax.ShapeDtypeStruct((count, width), jnp.bfloat16),
        scratch_shapes=[pltpu.VMEM((block, width), jnp.float32)],
        compiler_params=pltpu.CompilerParams(vmem_limit_bytes=48 * 1024 * 1024),
        cost_estimate=pl.CostEstimate(
            flops=6 * count * width * units * slots,
            bytes_accessed=4 * count * width + 6 * slots * width * units,
            transcendentals=count * units * slots,
        ),
    )(x, shares, gate_up, down_proj)


def run_batches(tokens, routes, weights, old_place, gate_up, down_proj):
    ep_count = lax.axis_size("ep")
    here = tokens.shape[0]
    slots_here = gate_up.shape[0]
    shares = weights / jnp.sum(weights, axis=1, keepdims=True)
    all_shares = lax.all_gather(shares, "ep", axis=0, tiled=True)
    all_routes = lax.all_gather(routes, "ep", axis=0, tiled=True)
    features = lax.all_gather(
        lax.all_gather(tokens, "ep", axis=0, tiled=True), "tp", axis=1, tiled=True
    )
    experts = lax.dynamic_slice_in_dim(old_place, lax.axis_index("ep") * slots_here, slots_here)
    slot_shares = jnp.sum(
        jnp.where(all_routes[None] == experts[:, None, None], all_shares[None], 0.0), axis=2
    )
    sums = expert_sums(features, slot_shares[:, :, None], gate_up, down_proj)
    result = lax.psum_scatter(sums, "tp", scatter_dimension=1, tiled=True)
    returned = lax.all_to_all(
        result.reshape(ep_count, here, -1), "ep", split_axis=0, concat_axis=0, tiled=True
    )
    return jnp.sum(returned.astype(jnp.float32), axis=0)


def migrate_first(gate_up, down_proj):
    return (
        lax.all_to_all(gate_up, "ep", split_axis=2, concat_axis=0, tiled=True),
        lax.all_to_all(down_proj, "ep", split_axis=2, concat_axis=0, tiled=True),
    )


def migrate_second(table_gate_up, table_down, new_place, old_slot):
    members = (
        new_place[:, None] == jnp.arange(old_slot.shape[0], dtype=jnp.int32)[None, :]
    ).astype(jnp.int32)
    source = jnp.sum(members * old_slot[None, :], axis=1)
    return (
        lax.all_to_all(table_gate_up[source], "ep", split_axis=0, concat_axis=2, tiled=True),
        lax.all_to_all(table_down[source], "ep", split_axis=0, concat_axis=2, tiled=True),
    )


def head_norm(values, gain):
    mean_sq = jnp.mean(values * values, axis=-1, keepdims=True)
    return values * lax.rsqrt(mean_sq + 1e-06) * gain


def apply_rope(values, positions):
    half = HEAD_DIM // 2
    inverse = jnp.exp(jnp.arange(half, dtype=jnp.float32) * (-2.0 / HEAD_DIM) * math.log(50000.0))
    angle = positions.astype(jnp.float32)[:, None] * inverse[None, :]
    cosine = jnp.cos(angle)[:, None, :]
    sine = jnp.sin(angle)[:, None, :]
    first = values[..., :half]
    second = values[..., half:]
    return jnp.concatenate(
        [first * cosine - second * sine, second * cosine + first * sine], axis=-1
    )


def on_device(
    tokens_first,
    routes_first,
    weights_first,
    tokens_second,
    stream_second,
    routes_second,
    weights_second,
    old_place,
    new_place,
    gate_up,
    down_proj,
    attn_gain,
    qkv_weight,
    query_gain,
    key_gain,
    positions,
):
    experts_range = jnp.arange(EXPERTS, dtype=jnp.int32)
    old_slot = jnp.zeros((EXPERTS,), jnp.int32).at[old_place].set(experts_range)
    table_gate_up, table_down = migrate_first(gate_up, down_proj)
    count = tokens_first.shape[0]
    tokens = jnp.concatenate([tokens_first, tokens_second], axis=0)
    tokens, table_down = lax.optimization_barrier((tokens, table_down))
    mixed = run_batches(
        tokens,
        jnp.concatenate([routes_first, routes_second], axis=0),
        jnp.concatenate([weights_first, weights_second], axis=0),
        old_place,
        gate_up,
        down_proj,
    )
    new_gate_up, new_down = migrate_second(table_gate_up, table_down, new_place, old_slot)
    output_first = mixed[:count].astype(jnp.bfloat16)
    mixed_second = mixed[count:]
    stream = stream_second.astype(jnp.float32) + mixed_second
    squares = lax.psum(jnp.sum(stream * stream, axis=1), "tp")
    normed = (stream * lax.rsqrt(squares / D + 1e-06)[:, None] * attn_gain[None, :]).astype(
        jnp.bfloat16
    )
    flat_weight = qkv_weight.reshape(qkv_weight.shape[0], -1)
    tokens_count = normed.shape[0]
    projected = jnp.dot(
        lax.all_gather(normed, "tp", axis=1, tiled=True),
        flat_weight,
        preferred_element_type=jnp.float32,
    )
    heads_here = flat_weight.shape[1] // (3 * HEAD_DIM)
    projected = projected.reshape(tokens_count, 3, heads_here, HEAD_DIM)
    query_heads = head_norm(projected[:, 0], query_gain)
    key_heads = head_norm(projected[:, 1], key_gain)
    query_rows = apply_rope(query_heads, positions).reshape(tokens_count, -1).astype(jnp.bfloat16)
    key_rows = apply_rope(key_heads, positions).reshape(tokens_count, -1).astype(jnp.bfloat16)
    value_rows = projected[:, 2].reshape(tokens_count, -1).astype(jnp.bfloat16)
    return (output_first, query_rows, key_rows, value_rows, new_gate_up, new_down)


def solution(mesh):
    placed = (
        P("ep", "tp"),
        P("ep", None),
        P("ep", None),
        P("ep", "tp"),
        P("ep", "tp"),
        P("ep", None),
        P("ep", None),
        P(),
        P(),
        P("ep", None, None, "tp"),
        P("ep", "tp", None),
        P("tp"),
        P(None, None, "tp"),
        P(),
        P(),
        P("ep"),
    )
    return jax.shard_map(
        on_device,
        mesh=mesh,
        in_specs=placed,
        out_specs=(
            P("ep", "tp"),
            P("ep", "tp"),
            P("ep", "tp"),
            P("ep", "tp"),
            P("ep", None, None, "tp"),
            P("ep", "tp", None),
        ),
        check_vma=False,
    )
```

```python
import math

import jax
import jax.numpy as jnp
from jax import lax
from jax.experimental import pallas as pl
from jax.experimental.pallas import tpu as pltpu
from jax.sharding import PartitionSpec as P

D = 2048
EXPERTS = 64
HEAD_DIM = 128


def expert_body(x_ref, share_ref, gate_up_ref, down_ref, out_ref, total):
    slot = pl.program_id(1)

    @pl.when(slot == 0)
    def _():
        total[...] = jnp.zeros_like(total)

    rows = 256 if x_ref.shape[0] % 256 == 0 else 48

    def step(i, carry):
        at = pl.ds(pl.multiple_of(i * rows, rows), rows)
        x = x_ref[at, :]
        gate_part = jnp.dot(x, gate_up_ref[0, 0], preferred_element_type=jnp.float32)
        up_part = jnp.dot(x, gate_up_ref[0, 1], preferred_element_type=jnp.float32)
        hidden = gate_part / (1.0 + jnp.exp(-gate_part)) * up_part * share_ref[0, at, :]
        total[at, :] += jnp.dot(
            hidden.astype(jnp.bfloat16), down_ref[0], preferred_element_type=jnp.float32
        )
        return carry

    lax.fori_loop(0, x_ref.shape[0] // rows, step, 0)

    @pl.when(slot == pl.num_programs(1) - 1)
    def _():
        out_ref[...] = total[...].astype(jnp.bfloat16)


def expert_sums(x, shares, gate_up, down_proj):
    count, width = x.shape
    slots, _, _, units = gate_up.shape
    block = 768 if count % 768 == 0 else count
    return pl.pallas_call(
        expert_body,
        grid=(count // block, slots),
        in_specs=[
            pl.BlockSpec((block, width), lambda i, s: (i, 0)),
            pl.BlockSpec((1, block, 1), lambda i, s: (s, i, 0)),
            pl.BlockSpec((1, 2, width, units), lambda i, s: (s, 0, 0, 0)),
            pl.BlockSpec((1, units, width), lambda i, s: (s, 0, 0)),
        ],
        out_specs=pl.BlockSpec((block, width), lambda i, s: (i, 0)),
        out_shape=jax.ShapeDtypeStruct((count, width), jnp.bfloat16),
        scratch_shapes=[pltpu.VMEM((block, width), jnp.float32)],
        compiler_params=pltpu.CompilerParams(vmem_limit_bytes=48 * 1024 * 1024),
        cost_estimate=pl.CostEstimate(
            flops=6 * count * width * units * slots,
            bytes_accessed=4 * count * width + 6 * slots * width * units,
            transcendentals=count * units * slots,
        ),
    )(x, shares, gate_up, down_proj)


def run_batches(tokens, routes, weights, old_place, gate_up, down_proj):
    slots_here = gate_up.shape[0]
    shares = weights / jnp.sum(weights, axis=1, keepdims=True)
    choices = lax.all_gather(
        jnp.concatenate([shares, routes.astype(jnp.float32)], axis=1), "ep", axis=0, tiled=True
    )
    all_shares = choices[:, : shares.shape[1]]
    all_routes = choices[:, shares.shape[1] :].astype(jnp.int32)
    features = lax.all_gather(
        lax.all_gather(tokens, "ep", axis=0, tiled=True), "tp", axis=1, tiled=True
    )
    experts = lax.dynamic_slice_in_dim(old_place, lax.axis_index("ep") * slots_here, slots_here)
    slot_shares = jnp.sum(
        jnp.where(all_routes[None] == experts[:, None, None], all_shares[None], 0.0), axis=2
    )
    sums = expert_sums(features, slot_shares[:, :, None], gate_up, down_proj)
    result = lax.psum_scatter(sums, "tp", scatter_dimension=1, tiled=True)
    return lax.psum_scatter(result, "ep", scatter_dimension=0, tiled=True).astype(jnp.float32)


def migrate_first(gate_up, down_proj):
    return (
        lax.all_to_all(gate_up, "ep", split_axis=2, concat_axis=0, tiled=True),
        lax.all_to_all(down_proj, "ep", split_axis=2, concat_axis=0, tiled=True),
    )


def migrate_second(table_gate_up, table_down, new_place, old_slot):
    members = (
        new_place[:, None] == jnp.arange(old_slot.shape[0], dtype=jnp.int32)[None, :]
    ).astype(jnp.int32)
    source = jnp.sum(members * old_slot[None, :], axis=1)
    return (
        lax.all_to_all(table_gate_up[source], "ep", split_axis=0, concat_axis=2, tiled=True),
        lax.all_to_all(table_down[source], "ep", split_axis=0, concat_axis=2, tiled=True),
    )


def head_norm(values, gain):
    mean_sq = jnp.mean(values * values, axis=-1, keepdims=True)
    return values * lax.rsqrt(mean_sq + 1e-06) * gain


def apply_rope(values, positions):
    half = HEAD_DIM // 2
    inverse = jnp.exp(jnp.arange(half, dtype=jnp.float32) * (-2.0 / HEAD_DIM) * math.log(50000.0))
    angle = positions.astype(jnp.float32)[:, None] * inverse[None, :]
    cosine = jnp.cos(angle)[:, None, :]
    sine = jnp.sin(angle)[:, None, :]
    first = values[..., :half]
    second = values[..., half:]
    return jnp.concatenate(
        [first * cosine - second * sine, second * cosine + first * sine], axis=-1
    )


def on_device(
    tokens_first,
    routes_first,
    weights_first,
    tokens_second,
    stream_second,
    routes_second,
    weights_second,
    old_place,
    new_place,
    gate_up,
    down_proj,
    attn_gain,
    qkv_weight,
    query_gain,
    key_gain,
    positions,
):
    experts_range = jnp.arange(EXPERTS, dtype=jnp.int32)
    old_slot = jnp.zeros((EXPERTS,), jnp.int32).at[old_place].set(experts_range)
    table_gate_up, table_down = migrate_first(gate_up, down_proj)
    count = tokens_first.shape[0]
    tokens = jnp.concatenate([tokens_first, tokens_second], axis=0)
    tokens, table_down = lax.optimization_barrier((tokens, table_down))
    mixed = run_batches(
        tokens,
        jnp.concatenate([routes_first, routes_second], axis=0),
        jnp.concatenate([weights_first, weights_second], axis=0),
        old_place,
        gate_up,
        down_proj,
    )
    new_gate_up, new_down = migrate_second(table_gate_up, table_down, new_place, old_slot)
    output_first = mixed[:count].astype(jnp.bfloat16)
    mixed_second = mixed[count:]
    stream = stream_second.astype(jnp.float32) + mixed_second
    squares = lax.psum(jnp.sum(stream * stream, axis=1), "tp")
    normed = (stream * lax.rsqrt(squares / D + 1e-06)[:, None] * attn_gain[None, :]).astype(
        jnp.bfloat16
    )
    flat_weight = qkv_weight.reshape(qkv_weight.shape[0], -1)
    tokens_count = normed.shape[0]
    projected = jnp.dot(
        lax.all_gather(normed, "tp", axis=1, tiled=True),
        flat_weight,
        preferred_element_type=jnp.float32,
    )
    heads_here = flat_weight.shape[1] // (3 * HEAD_DIM)
    projected = projected.reshape(tokens_count, 3, heads_here, HEAD_DIM)
    query_heads = head_norm(projected[:, 0], query_gain)
    key_heads = head_norm(projected[:, 1], key_gain)
    query_rows = apply_rope(query_heads, positions).reshape(tokens_count, -1).astype(jnp.bfloat16)
    key_rows = apply_rope(key_heads, positions).reshape(tokens_count, -1).astype(jnp.bfloat16)
    value_rows = projected[:, 2].reshape(tokens_count, -1).astype(jnp.bfloat16)
    return (output_first, query_rows, key_rows, value_rows, new_gate_up, new_down)


def solution(mesh):
    placed = (
        P("ep", "tp"),
        P("ep", None),
        P("ep", None),
        P("ep", "tp"),
        P("ep", "tp"),
        P("ep", None),
        P("ep", None),
        P(),
        P(),
        P("ep", None, None, "tp"),
        P("ep", "tp", None),
        P("tp"),
        P(None, None, "tp"),
        P(),
        P(),
        P("ep"),
    )
    return jax.shard_map(
        on_device,
        mesh=mesh,
        in_specs=placed,
        out_specs=(
            P("ep", "tp"),
            P("ep", "tp"),
            P("ep", "tp"),
            P("ep", "tp"),
            P("ep", None, None, "tp"),
            P("ep", "tp", None),
        ),
        check_vma=False,
    )
```

```python
import math

import jax
import jax.numpy as jnp
from jax import lax
from jax.experimental import pallas as pl
from jax.experimental.pallas import tpu as pltpu
from jax.sharding import PartitionSpec as P

D = 2048
EXPERTS = 64
HEAD_DIM = 128


def expert_body(x_ref, share_ref, gate_up_ref, down_ref, out_ref, total):
    slot = pl.program_id(1)

    @pl.when(slot == 0)
    def _():
        total[...] = jnp.zeros_like(total)

    rows = 256 if x_ref.shape[0] % 256 == 0 else 48

    def step(i, carry):
        at = pl.ds(pl.multiple_of(i * rows, rows), rows)
        x = x_ref[at, :]
        gate_part = jnp.dot(x, gate_up_ref[0, 0], preferred_element_type=jnp.float32)
        up_part = jnp.dot(x, gate_up_ref[0, 1], preferred_element_type=jnp.float32)
        hidden = gate_part / (1.0 + jnp.exp(-gate_part)) * up_part * share_ref[0, at, :]
        total[at, :] += jnp.dot(
            hidden.astype(jnp.bfloat16), down_ref[0], preferred_element_type=jnp.float32
        )
        return carry

    lax.fori_loop(0, x_ref.shape[0] // rows, step, 0)

    @pl.when(slot == pl.num_programs(1) - 1)
    def _():
        out_ref[...] = total[...].astype(jnp.bfloat16)


def expert_sums(x, shares, gate_up, down_proj):
    count, width = x.shape
    slots, _, _, units = gate_up.shape
    block = 768 if count % 768 == 0 else count
    return pl.pallas_call(
        expert_body,
        grid=(count // block, slots),
        in_specs=[
            pl.BlockSpec((block, width), lambda i, s: (i, 0)),
            pl.BlockSpec((1, block, 1), lambda i, s: (s, i, 0)),
            pl.BlockSpec((1, 2, width, units), lambda i, s: (s, 0, 0, 0)),
            pl.BlockSpec((1, units, width), lambda i, s: (s, 0, 0)),
        ],
        out_specs=pl.BlockSpec((block, width), lambda i, s: (i, 0)),
        out_shape=jax.ShapeDtypeStruct((count, width), jnp.bfloat16),
        scratch_shapes=[pltpu.VMEM((block, width), jnp.float32)],
        compiler_params=pltpu.CompilerParams(vmem_limit_bytes=48 * 1024 * 1024),
        cost_estimate=pl.CostEstimate(
            flops=6 * count * width * units * slots,
            bytes_accessed=4 * count * width + 6 * slots * width * units,
            transcendentals=count * units * slots,
        ),
    )(x, shares, gate_up, down_proj)


def gather_rows(values):
    count = lax.axis_size("ep")
    spread = jnp.broadcast_to(values[None], (count,) + values.shape)
    gathered = lax.all_to_all(spread, "ep", split_axis=0, concat_axis=0, tiled=True)
    return gathered.reshape((count * values.shape[0],) + values.shape[1:])


def expert_mixture(features, choices, old_place, gate_up, down_proj):
    slots_here = gate_up.shape[0]
    top = choices.shape[1] // 2
    all_shares = choices[:, :top]
    all_routes = choices[:, top:].astype(jnp.int32)
    experts = lax.dynamic_slice_in_dim(old_place, lax.axis_index("ep") * slots_here, slots_here)
    slot_shares = jnp.sum(
        jnp.where(all_routes[None] == experts[:, None, None], all_shares[None], 0.0), axis=2
    )
    features = lax.all_gather(features, "tp", axis=1, tiled=True)
    sums = expert_sums(features, slot_shares[:, :, None], gate_up, down_proj)
    return lax.psum_scatter(sums, "tp", scatter_dimension=1, tiled=True)


def exchange(blocks):
    return lax.all_to_all(blocks, "ep", split_axis=0, concat_axis=0, tiled=True)


def by_destination(gate_up):
    count = lax.axis_size("ep")
    slots, pair, width, units = gate_up.shape
    return gate_up.reshape(slots, pair, count, width // count, units).transpose(2, 0, 1, 3, 4)


def slot_source(new_place, old_slot):
    members = (
        new_place[:, None] == jnp.arange(old_slot.shape[0], dtype=jnp.int32)[None, :]
    ).astype(jnp.int32)
    return jnp.sum(members * old_slot[None, :], axis=1)


def head_norm(values, gain):
    mean_sq = jnp.mean(values * values, axis=-1, keepdims=True)
    return values * lax.rsqrt(mean_sq + 1e-06) * gain


def apply_rope(values, positions):
    half = HEAD_DIM // 2
    inverse = jnp.exp(jnp.arange(half, dtype=jnp.float32) * (-2.0 / HEAD_DIM) * math.log(50000.0))
    angle = positions.astype(jnp.float32)[:, None] * inverse[None, :]
    cosine = jnp.cos(angle)[:, None, :]
    sine = jnp.sin(angle)[:, None, :]
    first = values[..., :half]
    second = values[..., half:]
    return jnp.concatenate(
        [first * cosine - second * sine, second * cosine + first * sine], axis=-1
    )


def on_device(
    tokens_first,
    routes_first,
    weights_first,
    tokens_second,
    stream_second,
    routes_second,
    weights_second,
    old_place,
    new_place,
    gate_up,
    down_proj,
    attn_gain,
    qkv_weight,
    query_gain,
    key_gain,
    positions,
):
    experts_range = jnp.arange(EXPERTS, dtype=jnp.int32)
    old_slot = jnp.zeros((EXPERTS,), jnp.int32).at[old_place].set(experts_range)
    source = slot_source(new_place, old_slot)
    ep_count = lax.axis_size("ep")
    count = tokens_first.shape[0]
    tokens = jnp.concatenate([tokens_first, tokens_second], axis=0)
    routes = jnp.concatenate([routes_first, routes_second], axis=0)
    weights = jnp.concatenate([weights_first, weights_second], axis=0)
    shares = weights / jnp.sum(weights, axis=1, keepdims=True)
    choices = gather_rows(jnp.concatenate([shares, routes.astype(jnp.float32)], axis=1))
    features = gather_rows(tokens)

    send_gate_up = by_destination(gate_up)
    send_down, features, choices = lax.optimization_barrier((down_proj, features, choices))
    table_down = lax.all_to_all(send_down, "ep", split_axis=2, concat_axis=0, tiled=True)
    features, choices, table_down = lax.optimization_barrier((features, choices, table_down))
    table_gate_up = exchange(send_gate_up)
    sums = expert_mixture(features, choices, old_place, gate_up, down_proj)
    sums, table_gate_up = lax.optimization_barrier((sums, table_gate_up))
    returned = exchange(sums.reshape(ep_count, 2 * count, -1))
    returned, table_gate_up = lax.optimization_barrier((returned, table_gate_up))
    mixed = jnp.sum(returned.astype(jnp.float32), axis=0)
    table_gate_up = table_gate_up.reshape((-1,) + table_gate_up.shape[2:])
    back_down = exchange(table_down[source].reshape((ep_count, -1) + table_down.shape[1:]))
    back_gate_up = exchange(
        table_gate_up[source].reshape((ep_count, -1) + table_gate_up.shape[1:])
    )
    new_down = back_down.transpose(1, 2, 0, 3).reshape((-1,) + down_proj.shape[1:])
    new_gate_up = back_gate_up.transpose(1, 2, 0, 3, 4).reshape((-1,) + gate_up.shape[1:])
    output_first = mixed[:count].astype(jnp.bfloat16)
    mixed_second = mixed[count:]
    stream = stream_second.astype(jnp.float32) + mixed_second
    squares = lax.psum(jnp.sum(stream * stream, axis=1), "tp")
    normed = (stream * lax.rsqrt(squares / D + 1e-06)[:, None] * attn_gain[None, :]).astype(
        jnp.bfloat16
    )
    flat_weight = qkv_weight.reshape(qkv_weight.shape[0], -1)
    tokens_count = normed.shape[0]
    projected = jnp.dot(
        lax.all_gather(normed, "tp", axis=1, tiled=True),
        flat_weight,
        preferred_element_type=jnp.float32,
    )
    heads_here = flat_weight.shape[1] // (3 * HEAD_DIM)
    projected = projected.reshape(tokens_count, 3, heads_here, HEAD_DIM)
    query_heads = head_norm(projected[:, 0], query_gain)
    key_heads = head_norm(projected[:, 1], key_gain)
    query_rows = apply_rope(query_heads, positions).reshape(tokens_count, -1).astype(jnp.bfloat16)
    key_rows = apply_rope(key_heads, positions).reshape(tokens_count, -1).astype(jnp.bfloat16)
    value_rows = projected[:, 2].reshape(tokens_count, -1).astype(jnp.bfloat16)
    return (output_first, query_rows, key_rows, value_rows, new_gate_up, new_down)


def solution(mesh):
    placed = (
        P("ep", "tp"),
        P("ep", None),
        P("ep", None),
        P("ep", "tp"),
        P("ep", "tp"),
        P("ep", None),
        P("ep", None),
        P(),
        P(),
        P("ep", None, None, "tp"),
        P("ep", "tp", None),
        P("tp"),
        P(None, None, "tp"),
        P(),
        P(),
        P("ep"),
    )
    return jax.shard_map(
        on_device,
        mesh=mesh,
        in_specs=placed,
        out_specs=(
            P("ep", "tp"),
            P("ep", "tp"),
            P("ep", "tp"),
            P("ep", "tp"),
            P("ep", None, None, "tp"),
            P("ep", "tp", None),
        ),
        check_vma=False,
    )
```
